32 devices in a mesh: grp: 2 (over y), seq: 4 (over x, core), lab: 4 (over z).
Axes of the slice: x: 2, y: 2, z: 4, core: 2. Of those that a mesh axis runs over, the one named last changes fastest.
Arguments:
- hidden: bfloat16 [6144, 4096], P(('grp', 'seq'), 'lab'), parts along dimension 0, may hold values from -6 to 6
- proj_weight: bfloat16 [4096, 256], P('lab'), may hold values from -0.09375 to 0.09375
- queries: bfloat16 [9216, 256], P('lab'), may hold values from -0.25 to 0.25
- code_weight: bfloat16 [9216, 256], P('lab'), may hold values from -4 to 4
- code_bias: float32 [9216], P('lab'), may hold values from -0.5 to 0.5
- labels: int32 [4, 9216], P('grp', 'lab'), parts along dimension 0, may hold values 0 or 1
- code_counts: int32 [8, 9216], P(('grp', 'seq'), 'lab'), parts along dimension 0, may hold values from 0 to 119, as said below
Outputs:
- note_loss: float32 [4], P('grp'), parts along dimension 0
- grad_hidden: bfloat16 [6144, 4096], P(('grp', 'seq'), 'lab'), parts along dimension 0
- grad_proj: bfloat16 [8192, 256], P(('grp', 'lab', 'seq')), parts along dimension 0
- grad_queries: bfloat16 [18432, 256], P(('grp', 'lab', 'seq')), parts along dimension 0
- grad_code_weight: bfloat16 [18432, 256], P(('grp', 'lab', 'seq')), parts along dimension 0
- grad_bias: float32 [18432], P(('grp', 'lab')), parts along dimension 0
The draws below stay inside these ranges and needn't reach their ends.
There are 2 independent parts, one for each index of `grp`. The reference program is written for one: setup_inputs(seed, part) draws one part's arguments, and reference() takes and returns one part's arrays. A program takes and returns all parts, laid end to end along the dimension named above; an argument that names none is the same for every part. Nothing has to cross between parts.
Inputs may be any that keep to these rules, and one draw needn't show every extreme that they name: `code_counts`: entry (i, c) counts the occurrences of code c in the part of the training corpus read by loader i.
All inputs are finite; a program needn't handle non-finite values. No bound on the sum of `labels` on one device may be relied on, other than what follows from the above.
Results may differ from the reference program's by a relative error of at most 0.025.
Values may be sent and summed in bfloat16 or wider, within the bound.
A program may use at most 64 MiB of HBM per device.

```python
import math
import jax
import jax.numpy as jnp
from jax import lax

D = 4096
E = 256
C_DEV = 2304
TOK_DEV = 768
NOTES = 2
CODES = 9216
TOKENS = 3072
CNT_ROWS = 4
N_SEQ = 4
N_LAB = 4


def draw_code_counts(key, part):
    row_index = jnp.arange(CNT_ROWS, dtype=jnp.int32)[:, None]
    ceiling = 20 + 40 * row_index // (CNT_ROWS - 1) + jnp.zeros((CNT_ROWS, CODES), jnp.int32)
    drawn = jax.random.randint(key, (CNT_ROWS, CODES), 0, 2 * ceiling + 2, dtype=jnp.int32)
    return jnp.minimum(drawn, 119)


def set_ends(values, stream_key, least, high):
    longest = values.shape.index(max(values.shape))
    spots = []
    for shift in (0, 1):
        where = [jax.random.randint(jax.random.fold_in(stream_key, axis), (), 0, length) for axis, length in enumerate(values.shape)]
        where[longest] = (where[longest] + shift) % values.shape[longest]
        spots.append(tuple(where))
    return values.at[spots[0]].set(least).at[spots[1]].set(high)


def block_levels(own_key, dims, shards, least, high):
    factor_of = 1.0
    for axis_at, parts in shards:
        steps = jax.random.uniform(jax.random.fold_in(jax.random.fold_in(own_key, 6), axis_at), (parts,), jnp.float32, least / len(shards), high / len(shards))
        factor_of = factor_of * jnp.repeat(jnp.exp(steps), dims[axis_at] // parts).reshape((-1,) + (1,) * (len(dims) - 1 - axis_at))
    return factor_of


def gaussian(own_key, dims, deviation, bound, cuts=(), kind=jnp.bfloat16):
    result = jax.random.normal(own_key, dims, jnp.float32) * deviation
    if len(cuts) > 0:
        result = block_levels(own_key, dims, cuts, -0.22, 0.18) * result
    return jnp.clip(result, min=-bound, max=bound).astype(kind)


def setup_inputs(seed: int = 0, part: int = 0) -> dict:
    seeds = jax.random.split(jax.random.key(seed), 8)
    own_keys = jax.random.split(jax.random.fold_in(seeds[7], part), 8)
    return {
        "hidden": gaussian(own_keys[0], (TOKENS, D), 1.0, 6.0, ((0, 4), (1, 4))),
        "proj_weight": gaussian(seeds[1], (D, E), D ** -0.5, 0.09375, ((0, 4),)),
        "queries": jnp.clip(jax.random.uniform(seeds[2], (CODES, E), jnp.float32, -0.25, 0.25) * block_levels(seeds[2], (CODES, E), ((0, 4),), -0.4, 0.0), -0.25, 0.25).astype(jnp.bfloat16),
        "code_weight": gaussian(seeds[3], (CODES, E), 1.0, 4.0, ((0, 4),)),
        "code_bias": jnp.clip(jax.random.uniform(seeds[4], (CODES,), jnp.float32, -0.5, 0.5) * block_levels(seeds[4], (CODES,), ((0, 4),), -0.4, 0.0), -0.5, 0.5),
        "labels": set_ends((jax.random.randint(own_keys[5], (NOTES, CODES), 0, 16) < 1).astype(jnp.int32), jax.random.fold_in(own_keys[5], 1), 0, 1),
        "code_counts": draw_code_counts(jax.random.fold_in(jax.random.fold_in(seeds[7], part), 71), part),
    }


balance_beta = 0.9999
HIGH = lax.Precision.HIGHEST

def focal_loss(logit, target):
    prob = jax.nn.sigmoid(logit)
    return -(target * (1.0 - prob) * (1.0 - prob) * jax.nn.log_sigmoid(logit) + (1.0 - target) * prob * prob * jax.nn.log_sigmoid(-logit))

def rounded(value):
    return lax.optimization_barrier(value.astype(jnp.bfloat16)).astype(jnp.float32)

def to_blocks(table):
    return table.reshape(NOTES, N_LAB, C_DEV).transpose(1, 0, 2)

def reference(hidden, proj_weight, queries, code_weight, code_bias, labels, code_counts):
    pre = jnp.dot(hidden, proj_weight, preferred_element_type=jnp.float32)
    latent = jnp.tanh(pre).astype(jnp.bfloat16)
    latent_wide = latent.astype(jnp.float32)
    note_length = TOKENS // NOTES
    note_owner = jnp.arange(TOKENS, dtype=jnp.int32) // note_length
    member = (note_owner[None, :] == jnp.arange(NOTES, dtype=jnp.int32)[:, None]).astype(jnp.float32)
    query_blocks = queries.reshape(N_LAB, C_DEV, E)
    weight_blocks = code_weight.reshape(N_LAB, C_DEV, E)

    def attend(query_rows, weight_rows):
        scores = jnp.einsum('ce,te->ct', query_rows.astype(jnp.float32), latent_wide, precision=HIGH)
        values = jnp.einsum('ce,te->ct', weight_rows.astype(jnp.float32), latent_wide, precision=HIGH)
        return (jnp.exp(scores), values)

    def forward_block(block_pair):
        weights, values = attend(block_pair[0], block_pair[1])
        denominator = jnp.einsum('ct,nt->nc', weights, member, precision=HIGH)
        numerator = jnp.einsum('ct,nt->nc', weights * values, member, precision=HIGH)
        return (denominator, numerator)
    denominator_blocks, numerator_blocks = lax.map(forward_block, (query_blocks, weight_blocks))
    denominator = denominator_blocks.transpose(1, 0, 2).reshape(NOTES, CODES)
    numerator = numerator_blocks.transpose(1, 0, 2).reshape(NOTES, CODES)
    mean_value = numerator / denominator
    logits = mean_value + code_bias[None, :]
    occurrences = 1.0 + lax.optimization_barrier(jnp.sum(code_counts.astype(jnp.float32), 0))
    class_weight = (1.0 - balance_beta) / -jnp.expm1(occurrences * math.log(balance_beta))
    targets = labels.astype(jnp.float32)
    focal_value, pullback = jax.vjp(lambda point: focal_loss(point, targets), logits)
    focal_grad = pullback(jnp.ones_like(logits))[0]
    factor = CODES / jnp.sum(class_weight)
    note_loss = factor * lax.optimization_barrier(jnp.sum(focal_value * class_weight[None, :], 1))
    logit_grad = factor * class_weight[None, :] * focal_grad
    grad_bias = lax.optimization_barrier(jnp.sum(logit_grad, 0))

    def backward_block(total, blocks):
        query_rows, weight_rows, grad_rows, denom_rows, mean_rows = blocks
        weights, values = attend(query_rows, weight_rows)
        denom_tok = jnp.einsum('nc,nt->ct', denom_rows, member, precision=HIGH)
        grad_tok = jnp.einsum('nc,nt->ct', grad_rows, member, precision=HIGH)
        mean_tok = jnp.einsum('nc,nt->ct', mean_rows, member, precision=HIGH)
        value_part = weights / denom_tok * grad_tok
        score_part = value_part * (values - mean_tok)
        value_grad = rounded(value_part)
        score_grad = rounded(score_part)
        total = total + jnp.einsum('ct,ce->te', score_grad, query_rows.astype(jnp.float32), precision=HIGH)
        total = total + jnp.einsum('ct,ce->te', value_grad, weight_rows.astype(jnp.float32), precision=HIGH)
        latent_split = latent_wide.reshape(N_SEQ, TOK_DEV, E)
        query_terms = jnp.einsum('cst,ste->sce', score_grad.reshape(C_DEV, N_SEQ, TOK_DEV), latent_split, precision=HIGH)
        weight_terms = jnp.einsum('cst,ste->sce', value_grad.reshape(C_DEV, N_SEQ, TOK_DEV), latent_split, precision=HIGH)
        query_sum = lax.optimization_barrier(jnp.sum(rounded(query_terms), 0)).astype(jnp.bfloat16)
        weight_sum = lax.optimization_barrier(jnp.sum(rounded(weight_terms), 0)).astype(jnp.bfloat16)
        return (total, (query_sum, weight_sum))
    latent_grad, (query_parts, weight_parts) = lax.scan(backward_block, jnp.zeros((TOKENS, E), jnp.float32), (query_blocks, weight_blocks, to_blocks(logit_grad), to_blocks(denominator), to_blocks(mean_value)))
    grad_queries = query_parts.reshape(CODES, E)
    grad_code_weight = weight_parts.reshape(CODES, E)
    pre_grad = (latent_grad * (1.0 - latent_wide * latent_wide)).astype(jnp.bfloat16)
    grad_hidden = jnp.dot(pre_grad, proj_weight.T, preferred_element_type=jnp.float32).astype(jnp.bfloat16)
    hidden_wide = hidden.astype(jnp.float32).reshape(N_SEQ, TOK_DEV, D)
    pre_grad_wide = pre_grad.astype(jnp.float32).reshape(N_SEQ, TOK_DEV, E)
    proj_terms = jnp.einsum('std,ste->sde', hidden_wide, pre_grad_wide, precision=HIGH)
    grad_proj = lax.optimization_barrier(jnp.sum(rounded(proj_terms), 0)).astype(jnp.bfloat16)
    return (note_loss, grad_hidden, grad_proj, grad_queries, grad_code_weight, grad_bias)
```

```python
import functools
import math

import jax
import jax.numpy as jnp
from jax import lax
from jax.experimental import pallas as pl
from jax.experimental.pallas import tpu as pltpu
from jax.sharding import PartitionSpec as P

balance_beta = 0.9999
MESH = pl.DeviceIdType.MESH
F32 = jnp.float32
BF16 = jnp.bfloat16


def expm1(x):
    series = jnp.ones_like(x)
    for order in range(10, 1, -1):
        series = 1.0 + x * series * (1.0 / order)
    return jnp.where(jnp.abs(x) < 0.5, x * series, jnp.exp(x) - 1.0)


def nt(a, b):
    return lax.dot_general(a, b, (((1,), (1,)), ((), ())), preferred_element_type=F32)


def nn(a, b):
    return jnp.dot(a, b, preferred_element_type=F32)


def rows(start, size, multiple):
    return pl.ds(pl.multiple_of(start, multiple), size)


def tile_of(size):
    return 256 if size % 256 == 0 else size


def kernel(
    S, L, all_codes,
    hidden, proj, queries, codew, bias, labels, counts,
    loss_out, gh_out, gp_out, gq_out, gw_out, gb_out,
    pre_b, rs1, lat, latT, w_s, v_s, tot, cnt, sc, den_n, mean_n, grad_n,
    sg_s, vg_s, acc, lg_b, rs2, pg, pgT,
    pq, pw, pp, q1, w1, p1, qs, ws, ps, q2, w2, p2,
    cnt_sem, tot_sem, sc_sem, rs1_sem, ag1_sem, rs2_sem, ag2_sem, st1_sem, st2_sem,
):
    T, D = hidden.shape
    C, E = queries.shape
    notes = labels.shape[0]
    X = S // 2
    sh = T // L
    me_s = lax.axis_index("seq")
    me_l = lax.axis_index("lab")
    x = me_s // 2
    c = lax.rem(me_s, 2)
    lab_peers = [lax.rem(me_l + d, L) for d in range(1, L)]
    seq_peers = [lax.rem(me_s + d, S) for d in range(1, S)]
    sent = []

    def send(src, dst, sems, index, device):
        copy = pltpu.make_async_remote_copy(
            src_ref=src,
            dst_ref=dst,
            send_sem=sems.at[(0,) + index],
            recv_sem=sems.at[(1,) + index],
            device_id=device,
            device_id_type=MESH,
        )
        copy.start()
        sent.append(copy)
        return copy

    barrier = pltpu.get_barrier_semaphore()
    for peer in lab_peers:
        pl.semaphore_signal(barrier, inc=1, device_id={"lab": peer}, device_id_type=MESH)
    for peer in seq_peers:
        pl.semaphore_signal(barrier, inc=1, device_id={"seq": peer}, device_id_type=MESH)

    cnt[me_s] = counts[...].astype(F32)
    tr = tile_of(T)

    @pl.loop(0, T // tr)
    def _(i):
        at = rows(i * tr, tr, tr)
        pre_b[at, :] = nn(hidden[at, :], proj[...]).astype(BF16)

    pl.semaphore_wait(barrier, S + L - 2)

    def share(j):
        return rows(j * sh, sh, 16)

    copies = [
        send(pre_b.at[share(p)], rs1.at[d], rs1_sem, (d,), {"lab": p})
        for d, p in enumerate(lab_peers)
    ]
    cnt_copies = [
        send(cnt.at[me_s], cnt.at[me_s], cnt_sem, (d,), {"seq": p})
        for d, p in enumerate(seq_peers)
    ]
    total = pre_b[share(me_l), :].astype(F32)
    for d, copy in enumerate(copies):
        copy.wait_recv()
        total = total + rs1[d].astype(F32)
    lat[share(me_l), :] = jnp.tanh(total).astype(BF16)
    copies = [
        send(lat.at[share(me_l)], lat.at[share(me_l)], ag1_sem, (d,), {"lab": p})
        for d, p in enumerate(lab_peers)
    ]
    for copy in copies:
        copy.wait_recv()

    tc = tile_of(C)

    @pl.loop(0, C // tc)
    def _(i):
        at = rows(i * tc, tc, tc)
        weights = jnp.exp(nt(lat[...], queries[at, :]))
        values = nt(lat[...], codew[at, :])
        w_s[:, at] = weights
        v_s[:, at] = values
        tot[me_s, 0:1, at] = jnp.sum(weights, 0, keepdims=True)
        tot[me_s, 1:2, at] = jnp.sum(weights * values, 0, keepdims=True)

    copies = [
        send(tot.at[me_s], tot.at[me_s], tot_sem, (d,), {"seq": p})
        for d, p in enumerate(seq_peers)
    ]
    latT[...] = lat[...].astype(F32).T.astype(BF16)
    for copy in cnt_copies:
        copy.wait_recv()
    occurrences = jnp.ones((1, C), F32)
    for s in range(S):
        occurrences = occurrences + cnt[s]
    class_weight = (1.0 - balance_beta) / -expm1(occurrences * math.log(balance_beta))
    for copy in copies:
        copy.wait_recv()
    losses = []
    bias_grad = jnp.zeros((1, C), F32)
    for n in range(notes):
        both = jnp.zeros((2, C), F32)
        for s in range(S):
            if s * notes // S == n:
                both = both + tot[s]
        inverse = 1.0 / both[0:1, :]
        mean = both[1:2, :] / both[0:1, :]
        logit = mean + bias[...]
        y = labels[n : n + 1, :].astype(F32)
        t = jnp.exp(-jnp.abs(logit))
        l1p = jnp.log1p(t)
        big = 1.0 / (1.0 + t)
        small = t / (1.0 + t)
        p = jnp.where(logit >= 0, big, small)
        q = jnp.where(logit >= 0, small, big)
        ls_pos = jnp.minimum(logit, 0.0) - l1p
        ls_neg = jnp.minimum(-logit, 0.0) - l1p
        focal = -(y * q * q * ls_pos + (1.0 - y) * p * p * ls_neg)
        slope = -(
            y * q * q * (q - 2.0 * p * ls_pos)
            + (1.0 - y) * p * p * (2.0 * q * ls_neg - p)
        )
        grad = class_weight * slope
        bias_grad = bias_grad + grad
        den_n[n] = inverse
        mean_n[n] = mean
        grad_n[n] = grad
        losses.append(jnp.sum(focal * class_weight, 1, keepdims=True))
    sc[me_l] = jnp.concatenate(
        [
            jnp.broadcast_to(value, (1, 128))
            for value in [jnp.sum(class_weight, 1, keepdims=True)] + losses
        ],
        axis=0,
    )
    sc_copies = [
        send(sc.at[me_l], sc.at[me_l], sc_sem, (d,), {"lab": p})
        for d, p in enumerate(lab_peers)
    ]

    note = me_s * notes // S
    acc[...] = jnp.zeros_like(acc)

    @pl.loop(0, C // tc)
    def _(i):
        at = rows(i * tc, tc, tc)
        value_part = w_s[:, at] * den_n[note, :, at] * grad_n[note, :, at]
        score_part = value_part * (v_s[:, at] - mean_n[note, :, at])
        vg = value_part.astype(BF16)
        sg = score_part.astype(BF16)
        vg_s[:, at] = vg
        sg_s[:, at] = sg
        acc[...] += nn(sg, queries[at, :]) + nn(vg, codew[at, :])

    lg_b[...] = acc[...].astype(BF16)
    rs2_copies = [
        send(lg_b.at[share(p)], rs2.at[d], rs2_sem, (d,), {"lab": p})
        for d, p in enumerate(lab_peers)
    ]

    sister = {"seq": x * 2 + (1 - c)}
    slots = list(range(1, X)) + [0]
    xs = [lax.rem(x + d, X) for d in range(X)]

    def chunk(ref, k):
        size = ref.shape[0] // S
        return rows(k * size, size, 16)

    def stage1(a, part, first):
        out = {}
        for d in slots:
            k = xs[d] * 2 + (1 - c)
            out[d] = send(part.at[chunk(part, k)], first.at[d], st1_sem, (a, d), sister)
        return out

    def stage2(a, part, first, mid, second, arrived):
        out = []
        for d in range(1, X):
            arrived[d].wait_recv()
            mine = part[chunk(part, xs[d] * 2 + c), :].astype(F32)
            mid[d - 1] = (mine + first[d].astype(F32)).astype(BF16)
            out.append(
                send(
                    mid.at[d - 1], second.at[d - 1], st2_sem, (a, d - 1),
                    {"seq": xs[d] * 2 + c},
                )
            )
        return out

    def finish(part, first, second, arrived, copies, scale, out):
        arrived[0].wait_recv()
        total = part[chunk(part, me_s), :].astype(F32) + first[0].astype(F32)
        for d, copy in enumerate(copies):
            copy.wait_recv()
            total = total + second[d].astype(F32)
        out[...] = (total * scale).astype(BF16)

    def code_part(grads, part):
        @pl.loop(0, C // tc)
        def _(i):
            at = rows(i * tc, tc, tc)
            part[at, :] = nn(latT[...], grads[:, at]).T.astype(BF16)

    code_part(sg_s, pq)
    q_first = stage1(0, pq, q1)
    code_part(vg_s, pw)
    w_first = stage1(1, pw, w1)
    q_second = stage2(0, pq, q1, qs, q2, q_first)

    for copy in sc_copies:
        copy.wait_recv()
    scalars = sc[0]
    for j in range(1, L):
        scalars = scalars + sc[j]
    factor = all_codes / scalars[0:1, 0:1]
    loss_out[...] = scalars[1 : 1 + notes, :] * factor
    gb_out[...] = bias_grad * factor

    total = lg_b[share(me_l), :].astype(F32)
    for d, copy in enumerate(rs2_copies):
        copy.wait_recv()
        total = total + rs2[d].astype(F32)
    wide = lat[share(me_l), :].astype(F32)
    pg[share(me_l), :] = (total * factor * (1.0 - wide * wide)).astype(BF16)
    ag2_copies = [
        send(pg.at[share(me_l)], pg.at[share(me_l)], ag2_sem, (d,), {"lab": p})
        for d, p in enumerate(lab_peers)
    ]
    w_second = stage2(1, pw, w1, ws, w2, w_first)
    for copy in ag2_copies:
        copy.wait_recv()
    pgT[...] = pg[...].astype(F32).T.astype(BF16)
    td = tile_of(D)

    @pl.loop(0, D // td)
    def _(i):
        at = rows(i * td, td, td)
        pp[at, :] = nn(pgT[...], hidden[:, at]).T.astype(BF16)

    p_first = stage1(2, pp, p1)

    @pl.loop(0, D // td)
    def _(i):
        at = rows(i * td, td, td)
        gh_out[:, at] = nt(pg[...], proj[at, :]).astype(BF16)

    p_second = stage2(2, pp, p1, ps, p2, p_first)
    finish(pq, q1, q2, q_first, q_second, factor, gq_out)
    finish(pw, w1, w2, w_first, w_second, factor, gw_out)
    finish(pp, p1, p2, p_first, p_second, 1.0, gp_out)
    for copy in sent:
        copy.wait_send()


def per_device(hidden, proj_weight, queries, code_weight, code_bias, labels, code_counts):
    L = lax.axis_size("lab")
    S = lax.axis_size("seq")
    X = S // 2
    T, D = hidden.shape
    C, E = queries.shape
    notes = labels.shape[0]
    sh = T // L
    vmem = pltpu.VMEM
    dma = pltpu.SemaphoreType.DMA
    scratch = [
        vmem((T, E), BF16),
        vmem((L - 1, sh, E), BF16),
        vmem((T, E), BF16),
        vmem((E, T), BF16),
        vmem((T, C), F32),
        vmem((T, C), F32),
        vmem((S, 2, C), F32),
        vmem((S, 1, C), F32),
        vmem((L, 1 + notes, 128), F32),
        vmem((notes, 1, C), F32),
        vmem((notes, 1, C), F32),
        vmem((notes, 1, C), F32),
        vmem((T, C), BF16),
        vmem((T, C), BF16),
        vmem((T, E), F32),
        vmem((T, E), BF16),
        vmem((L - 1, sh, E), BF16),
        vmem((T, E), BF16),
        vmem((E, T), BF16),
        vmem((C, E), BF16),
        vmem((C, E), BF16),
        vmem((D, E), BF16),
        vmem((X, C // S, E), BF16),
        vmem((X, C // S, E), BF16),
        vmem((X, D // S, E), BF16),
        vmem((X - 1, C // S, E), BF16),
        vmem((X - 1, C // S, E), BF16),
        vmem((X - 1, D // S, E), BF16),
        vmem((X - 1, C // S, E), BF16),
        vmem((X - 1, C // S, E), BF16),
        vmem((X - 1, D // S, E), BF16),
        dma((2, S - 1)),
        dma((2, S - 1)),
        dma((2, L - 1)),
        dma((2, L - 1)),
        dma((2, L - 1)),
        dma((2, L - 1)),
        dma((2, L - 1)),
        dma((2, 3, X)),
        dma((2, 3, X - 1)),
    ]
    whole = pl.BlockSpec(memory_space=pltpu.VMEM)
    loss, gh, gp, gq, gw, gb = pl.pallas_call(
        functools.partial(kernel, S, L, float(C * L)),
        out_shape=(
            jax.ShapeDtypeStruct((notes, 128), F32),
            jax.ShapeDtypeStruct((T, D), BF16),
            jax.ShapeDtypeStruct((D // S, E), BF16),
            jax.ShapeDtypeStruct((C // S, E), BF16),
            jax.ShapeDtypeStruct((C // S, E), BF16),
            jax.ShapeDtypeStruct((1, C), F32),
        ),
        in_specs=[whole] * 7,
        out_specs=(whole,) * 6,
        scratch_shapes=scratch,
        compiler_params=pltpu.CompilerParams(
            collective_id=0, has_side_effects=True, vmem_limit_bytes=56 * 1024 * 1024
        ),
    )(
        hidden, proj_weight, queries, code_weight, code_bias.reshape(1, C), labels, code_counts
    )
    return loss[:, 0], gh, gp, gq, gw, gb.reshape(C)


def solution(mesh):
    placed = (
        P(("grp", "seq"), "lab"),
        P("lab", None),
        P("lab", None),
        P("lab", None),
        P("lab"),
        P("grp", "lab"),
        P(("grp", "seq"), "lab"),
    )
    return jax.shard_map(
        per_device,
        mesh=mesh,
        in_specs=placed,
        out_specs=(
            P("grp"),
            P(("grp", "seq"), "lab"),
            P(("grp", "lab", "seq"), None),
            P(("grp", "lab", "seq"), None),
            P(("grp", "lab", "seq"), None),
            P(("grp", "lab")),
        ),
        check_vma=False,
    )
```

```python
import functools
import math

import jax
import jax.numpy as jnp
from jax import lax
from jax.experimental import pallas as pl
from jax.experimental.pallas import tpu as pltpu
from jax.sharding import PartitionSpec as P

balance_beta = 0.9999
MESH = pl.DeviceIdType.MESH
F32 = jnp.float32
BF16 = jnp.bfloat16


def expm1(x):
    series = jnp.ones_like(x)
    for order in range(10, 1, -1):
        series = 1.0 + x * series * (1.0 / order)
    return jnp.where(jnp.abs(x) < 0.5, x * series, jnp.exp(x) - 1.0)


def nt(a, b):
    return lax.dot_general(a, b, (((1,), (1,)), ((), ())), preferred_element_type=F32)


def nn(a, b):
    return jnp.dot(a, b, preferred_element_type=F32)


def rows(start, size, multiple):
    return pl.ds(pl.multiple_of(start, multiple), size)


def tile_of(size, most=768):
    for tile in (768, 512, 256):
        if tile <= most and size % tile == 0:
            return tile
    return size


def far_first(count):
    return sorted(range(1, count), key=lambda d: -min(d, count - d))


def kernel(
    S, L, all_codes,
    hidden_h, proj_h, queries_h, codew_h, bias, labels, counts,
    loss_out, pg_out, gp_out, gq_out, gw_out, gb_out,
    hidden, proj, queries, codew, load_sem, pre_b, rs1, lat, latT, w_s, v_s, tot, cnt, sc, den_n, mean_n, grad_n,
    sg_s, vg_s, acc, lg_b, rs2, pg, pgT,
    pq, pw, pp, q1, w1, p1, qs, ws, ps, q2, w2, p2,
    cnt_sem, tot_sem, sc_sem, rs1_sem, ag1_sem, rs2_sem, ag2_sem, st1_sem, st2_sem,
):
    T, D = hidden.shape
    C, E = queries.shape
    notes = labels.shape[0]
    X = S // 2
    sh = T // L
    me_s = lax.axis_index("seq")
    me_l = lax.axis_index("lab")
    x = me_s // 2
    c = lax.rem(me_s, 2)
    lab_peers = [lax.rem(me_l + d, L) for d in range(1, L)]
    seq_peers = [lax.rem(me_s + d, S) for d in range(1, S)]
    sent = []

    def send(src, dst, sems, index, device):
        copy = pltpu.make_async_remote_copy(
            src_ref=src,
            dst_ref=dst,
            send_sem=sems.at[(0,) + index],
            recv_sem=sems.at[(1,) + index],
            device_id=device,
            device_id_type=MESH,
        )
        copy.start()
        sent.append(copy)
        return copy

    barrier = pltpu.get_barrier_semaphore()
    for peer in lab_peers:
        pl.semaphore_signal(barrier, inc=1, device_id={"lab": peer}, device_id_type=MESH)
    for peer in seq_peers:
        pl.semaphore_signal(barrier, inc=1, device_id={"seq": peer}, device_id_type=MESH)

    loads = [
        pltpu.make_async_copy(src, dst, load_sem.at[k])
        for k, (src, dst) in enumerate(
            [(proj_h, proj), (hidden_h, hidden), (queries_h, queries), (codew_h, codew)]
        )
    ]
    for load in loads:
        load.start()
    cnt[me_s] = counts[...].astype(F32)
    loads[0].wait()
    loads[1].wait()

    def share(j):
        return rows(j * sh, sh, 16)

    def project(j):
        pre_b[share(j), :] = nn(hidden[share(j), :], proj[...]).astype(BF16)

    lab_order = far_first(L)
    copies = {}
    for k, d in enumerate(lab_order):
        p = lab_peers[d - 1]
        project(p)
        if k == 0:
            pl.semaphore_wait(barrier, S + L - 2)
        copies[d] = send(pre_b.at[share(p)], rs1.at[d - 1], rs1_sem, (d - 1,), {"lab": p})
    project(me_l)
    cnt_copies = [
        send(cnt.at[me_s], cnt.at[me_s], cnt_sem, (d,), {"seq": p})
        for d, p in enumerate(seq_peers)
    ]
    total = pre_b[share(me_l), :].astype(F32)
    for d in reversed(lab_order):
        copies[d].wait_recv()
        total = total + rs1[d - 1].astype(F32)
    lat[share(me_l), :] = jnp.tanh(total).astype(BF16)
    copies = {
        d: send(
            lat.at[share(me_l)], lat.at[share(me_l)], ag1_sem, (d - 1,), {"lab": lab_peers[d - 1]}
        )
        for d in lab_order
    }
    loads[2].wait()
    loads[3].wait()

    tc = tile_of(C)
    tot[me_s] = jnp.zeros((2, C), F32)

    def attend(j):
        block = lat[share(j), :]

        @pl.loop(0, C // tc)
        def _(i):
            at = rows(i * tc, tc, tc)
            weights = jnp.exp(nt(block, queries[at, :]))
            values = nt(block, codew[at, :])
            w_s[share(j), at] = weights
            v_s[share(j), at] = values
            tot[me_s, 0:1, at] += jnp.sum(weights, 0, keepdims=True)
            tot[me_s, 1:2, at] += jnp.sum(weights * values, 0, keepdims=True)

    attend(me_l)
    for d in reversed(lab_order):
        copies[d].wait_recv()
        attend(lax.rem(me_l + L - d, L))

    copies = [
        send(tot.at[me_s], tot.at[me_s], tot_sem, (d,), {"seq": p})
        for d, p in enumerate(seq_peers)
    ]
    latT[...] = lat[...].astype(F32).T.astype(BF16)
    for copy in cnt_copies:
        copy.wait_recv()
    occurrences = jnp.ones((1, C), F32)
    for s in range(S):
        occurrences = occurrences + cnt[s]
    class_weight = (1.0 - balance_beta) / -expm1(occurrences * math.log(balance_beta))
    for copy in copies:
        copy.wait_recv()
    losses = []
    bias_grad = jnp.zeros((1, C), F32)
    for n in range(notes):
        both = jnp.zeros((2, C), F32)
        for s in range(S):
            if s * notes // S == n:
                both = both + tot[s]
        inverse = 1.0 / both[0:1, :]
        mean = both[1:2, :] / both[0:1, :]
        logit = mean + bias[...][None, :]
        y = labels[n : n + 1, :].astype(F32)
        t = jnp.exp(-jnp.abs(logit))
        l1p = jnp.log1p(t)
        big = 1.0 / (1.0 + t)
        small = t / (1.0 + t)
        p = jnp.where(logit >= 0, big, small)
        q = jnp.where(logit >= 0, small, big)
        ls_pos = jnp.minimum(logit, 0.0) - l1p
        ls_neg = jnp.minimum(-logit, 0.0) - l1p
        focal = -(y * q * q * ls_pos + (1.0 - y) * p * p * ls_neg)
        slope = -(
            y * q * q * (q - 2.0 * p * ls_pos)
            + (1.0 - y) * p * p * (2.0 * q * ls_neg - p)
        )
        grad = class_weight * slope
        bias_grad = bias_grad + grad
        den_n[n] = inverse
        mean_n[n] = mean
        grad_n[n] = grad
        losses.append(jnp.sum(focal * class_weight, 1, keepdims=True))
    sc[me_l] = jnp.concatenate(
        [
            jnp.broadcast_to(value, (1, 128))
            for value in [jnp.sum(class_weight, 1, keepdims=True)] + losses
        ],
        axis=0,
    )
    sc_copies = [
        send(sc.at[me_l], sc.at[me_l], sc_sem, (d,), {"lab": p})
        for d, p in enumerate(lab_peers)
    ]

    note = me_s * notes // S
    sister = {"seq": x * 2 + (1 - c)}
    slots = list(range(1, X)) + [0]
    xs = [lax.rem(x + d, X) for d in range(X)]

    def chunk(ref, k):
        size = ref.shape[0] // S
        return rows(k * size, size, 16)

    def stage1(a, part, first):
        out = {}
        for d in slots:
            k = xs[d] * 2 + (1 - c)
            out[d] = send(part.at[chunk(part, k)], first.at[d], st1_sem, (a, d), sister)
        return out

    def stage2(a, part, first, mid, second, arrived):
        out = []
        for d in range(1, X):
            arrived[d].wait_recv()
            mine = part[chunk(part, xs[d] * 2 + c), :].astype(F32)
            mid[d - 1] = (mine + first[d].astype(F32)).astype(BF16)
            out.append(
                send(
                    mid.at[d - 1], second.at[d - 1], st2_sem, (a, d - 1),
                    {"seq": xs[d] * 2 + c},
                )
            )
        return out

    def finish(part, first, second, arrived, copies, scale, out):
        arrived[0].wait_recv()
        total = part[chunk(part, me_s), :].astype(F32) + first[0].astype(F32)
        for d, copy in enumerate(copies):
            copy.wait_recv()
            total = total + second[d].astype(F32)
        out[...] = (total * scale).astype(BF16)

    tw = tile_of(C, 256)

    def code_part(grads, part):
        @pl.loop(0, C // tw)
        def _(i):
            at = rows(i * tw, tw, tw)
            part[at, :] = nn(latT[...], grads[:, at]).T.astype(BF16)

    @pl.loop(0, C // tw)
    def _(i):
        at = rows(i * tw, tw, tw)
        value_part = w_s[:, at] * den_n[note, :, at] * grad_n[note, :, at]
        vg = value_part.astype(BF16)
        w_s[:, at] = value_part
        vg_s[:, at] = vg
        pw[at, :] = nn(latT[...], vg).T.astype(BF16)

    w_first = stage1(1, pw, w1)

    def latent_grad(j):
        acc[...] = jnp.zeros_like(acc)

        @pl.loop(0, C // tc)
        def _(i):
            at = rows(i * tc, tc, tc)
            score_part = w_s[share(j), at] * (v_s[share(j), at] - mean_n[note, :, at])
            sg = score_part.astype(BF16)
            sg_s[share(j), at] = sg
            acc[...] += nn(sg, queries[at, :]) + nn(vg_s[share(j), at], codew[at, :])

    rs2_copies = {}
    w_second = None
    for k, d in enumerate(lab_order):
        p = lab_peers[d - 1]
        latent_grad(p)
        lg_b[share(p), :] = acc[...].astype(BF16)
        rs2_copies[d] = send(lg_b.at[share(p)], rs2.at[d - 1], rs2_sem, (d - 1,), {"lab": p})
        if k == 0:
            w_second = stage2(1, pw, w1, ws, w2, w_first)
    latent_grad(me_l)
    code_part(sg_s, pq)
    q_first = stage1(0, pq, q1)

    for copy in sc_copies:
        copy.wait_recv()
    scalars = sc[0]
    for j in range(1, L):
        scalars = scalars + sc[j]
    factor = all_codes / scalars[0:1, 0:1]
    loss_out[...] = scalars[1 : 1 + notes, :] * factor
    gb_out[...] = bias_grad * factor

    total = acc[...]
    for d in reversed(lab_order):
        rs2_copies[d].wait_recv()
        total = total + rs2[d - 1].astype(F32)
    wide = lat[share(me_l), :].astype(F32)
    pg[share(me_l), :] = (total * factor * (1.0 - wide * wide)).astype(BF16)
    ag2_copies = [
        send(pg.at[share(me_l)], pg.at[share(me_l)], ag2_sem, (d,), {"lab": p})
        for d, p in enumerate(lab_peers)
    ]
    q_second = stage2(0, pq, q1, qs, q2, q_first)
    for copy in ag2_copies:
        copy.wait_recv()
    pgT[...] = pg[...].astype(F32).T.astype(BF16)
    td = tile_of(D, 256)

    @pl.loop(0, D // td)
    def _(i):
        at = rows(i * td, td, td)
        pp[at, :] = nn(pgT[...], hidden[:, at]).T.astype(BF16)

    p_first = stage1(2, pp, p1)

    pg_out[...] = pg[...]
    p_second = stage2(2, pp, p1, ps, p2, p_first)
    finish(pw, w1, w2, w_first, w_second, factor, gw_out)
    finish(pq, q1, q2, q_first, q_second, factor, gq_out)
    finish(pp, p1, p2, p_first, p_second, 1.0, gp_out)
    for copy in sent:
        copy.wait_send()


def finish_kernel(
    loss, pg, gp, gq, gw, gb, proj, loss_out, gh_out, gp_out, gq_out, gw_out, gb_out, gh, sem
):
    copies = []
    for k, (src, dst) in enumerate([(gp, gp_out), (gq, gq_out), (gw, gw_out)]):
        copies.append(pltpu.make_async_copy(src, dst, sem.at[k]))
        copies[-1].start()
    part = gh.shape[0] // 4
    for k in range(4):
        at = pl.ds(k * part, part)
        gh[at, :] = nt(pg[at, :], proj[...]).astype(BF16)
        copies.append(pltpu.make_async_copy(gh.at[at], gh_out.at[at], sem.at[3 + k]))
        copies[-1].start()
    gb_out[...] = gb[0, :]
    for n in range(loss_out.shape[0]):
        loss_out[n] = jnp.max(loss[n : n + 1, :])
    for copy in copies:
        copy.wait()


def per_device(hidden, proj_weight, queries, code_weight, code_bias, labels, code_counts):
    L = lax.axis_size("lab")
    S = lax.axis_size("seq")
    X = S // 2
    T, D = hidden.shape
    C, E = queries.shape
    notes = labels.shape[0]
    sh = T // L
    vmem = pltpu.VMEM
    dma = pltpu.SemaphoreType.DMA
    scratch = [
        vmem((T, D), BF16),
        vmem((D, E), BF16),
        vmem((C, E), BF16),
        vmem((C, E), BF16),
        dma((4,)),
        vmem((T, E), BF16),
        vmem((L - 1, sh, E), BF16),
        vmem((T, E), BF16),
        vmem((E, T), BF16),
        vmem((T, C), F32),
        vmem((T, C), F32),
        vmem((S, 2, C), F32),
        vmem((S, 1, C), F32),
        vmem((L, 1 + notes, 128), F32),
        vmem((notes, 1, C), F32),
        vmem((notes, 1, C), F32),
        vmem((notes, 1, C), F32),
        vmem((T, C), BF16),
        vmem((T, C), BF16),
        vmem((sh, E), F32),
        vmem((T, E), BF16),
        vmem((L - 1, sh, E), BF16),
        vmem((T, E), BF16),
        vmem((E, T), BF16),
        vmem((C, E), BF16),
        vmem((C, E), BF16),
        vmem((D, E), BF16),
        vmem((X, C // S, E), BF16),
        vmem((X, C // S, E), BF16),
        vmem((X, D // S, E), BF16),
        vmem((X - 1, C // S, E), BF16),
        vmem((X - 1, C // S, E), BF16),
        vmem((X - 1, D // S, E), BF16),
        vmem((X - 1, C // S, E), BF16),
        vmem((X - 1, C // S, E), BF16),
        vmem((X - 1, D // S, E), BF16),
        dma((2, S - 1)),
        dma((2, S - 1)),
        dma((2, L - 1)),
        dma((2, L - 1)),
        dma((2, L - 1)),
        dma((2, L - 1)),
        dma((2, L - 1)),
        dma((2, 3, X)),
        dma((2, 3, X - 1)),
    ]
    whole = pl.BlockSpec(memory_space=pltpu.VMEM)
    anywhere = pl.BlockSpec(memory_space=pl.ANY)
    shapes = dict(
        gp=jax.ShapeDtypeStruct((D // S, E), BF16),
        gq=jax.ShapeDtypeStruct((C // S, E), BF16),
        gw=jax.ShapeDtypeStruct((C // S, E), BF16),
    )
    loss, pg, gp, gq, gw, gb = pl.pallas_call(
        functools.partial(kernel, S, L, float(C * L)),
        out_shape=(
            jax.ShapeDtypeStruct((notes, 128), F32),
            jax.ShapeDtypeStruct((T, E), BF16),
            *shapes.values(),
            jax.ShapeDtypeStruct((1, C), F32),
        ),
        in_specs=[anywhere] * 4 + [whole] * 3,
        out_specs=(whole,) * 6,
        scratch_shapes=scratch,
        compiler_params=pltpu.CompilerParams(
            collective_id=0, has_side_effects=True, vmem_limit_bytes=56 * 1024 * 1024
        ),
    )(hidden, proj_weight, queries, code_weight, code_bias, labels, code_counts)
    return pl.pallas_call(
        finish_kernel,
        out_shape=(
            jax.ShapeDtypeStruct((notes,), F32),
            jax.ShapeDtypeStruct((T, D), BF16),
            *shapes.values(),
            jax.ShapeDtypeStruct((C,), F32),
        ),
        in_specs=[whole] * 7,
        out_specs=(
            pl.BlockSpec(memory_space=pltpu.SMEM),
            anywhere,
            anywhere,
            anywhere,
            anywhere,
            whole,
        ),
        scratch_shapes=[vmem((T, D), BF16), dma((7,))],
    )(loss, pg, gp, gq, gw, gb, proj_weight)


def solution(mesh):
    placed = (
        P(("grp", "seq"), "lab"),
        P("lab", None),
        P("lab", None),
        P("lab", None),
        P("lab"),
        P("grp", "lab"),
        P(("grp", "seq"), "lab"),
    )
    return jax.shard_map(
        per_device,
        mesh=mesh,
        in_specs=placed,
        out_specs=(
            P("grp"),
            P(("grp", "seq"), "lab"),
            P(("grp", "lab", "seq"), None),
            P(("grp", "lab", "seq"), None),
            P(("grp", "lab", "seq"), None),
            P(("grp", "lab")),
        ),
        check_vma=False,
    )
```

```python
import functools
import math

import jax
import jax.numpy as jnp
from jax import lax
from jax.experimental import pallas as pl
from jax.experimental.pallas import tpu as pltpu
from jax.sharding import PartitionSpec as P

balance_beta = 0.9999
MESH = pl.DeviceIdType.MESH
F32 = jnp.float32
BF16 = jnp.bfloat16


def expm1(x):
    series = jnp.ones_like(x)
    for order in range(10, 1, -1):
        series = 1.0 + x * series * (1.0 / order)
    return jnp.where(jnp.abs(x) < 0.5, x * series, jnp.exp(x) - 1.0)


def nt(a, b):
    return lax.dot_general(a, b, (((1,), (1,)), ((), ())), preferred_element_type=F32)


def nn(a, b):
    return jnp.dot(a, b, preferred_element_type=F32)


def rows(start, size, multiple):
    return pl.ds(pl.multiple_of(start, multiple), size)


def tile_of(size, most=768):
    for tile in (768, 512, 256):
        if tile <= most and size % tile == 0:
            return tile
    return size


def far_first(count):
    return sorted(range(1, count), key=lambda d: -min(d, count - d))


def kernel(
    S, L, all_codes,
    hidden_h, proj_h, queries_h, codew_h, bias, labels, counts,
    loss_out, pg_out, gp_out, gq_out, gw_out, gb_out,
    hidden, proj, queries, codew, load_sem, pre_b, rs1, lat, latT, w_s, v_s, tot, cnt, sc, den_n, mean_n, grad_n,
    sg_s, vg_s, acc, lg_b, rs2, pg, pgT,
    pq, pw, pp, q1, w1, p1, qs, ws, ps, q2, w2, p2,
    cnt_sem, tot_sem, sc_sem, rs1_sem, ag1_sem, rs2_sem, ag2_sem, st1_sem, st2_sem,
):
    T, D = hidden.shape
    C, E = queries.shape
    notes = labels.shape[0]
    X = S // 2
    sh = T // L
    me_s = lax.axis_index("seq")
    me_l = lax.axis_index("lab")
    x = me_s // 2
    c = lax.rem(me_s, 2)
    lab_peers = [lax.rem(me_l + d, L) for d in range(1, L)]
    seq_peers = [lax.rem(me_s + d, S) for d in range(1, S)]
    sent = []
    sent_if = []

    def send(src, dst, sems, index, device):
        copy = pltpu.make_async_remote_copy(
            src_ref=src,
            dst_ref=dst,
            send_sem=sems.at[(0,) + index],
            recv_sem=sems.at[(1,) + index],
            device_id=device,
            device_id_type=MESH,
        )
        copy.start()
        sent.append(copy)
        return copy

    line = L == 4
    gather_order = [2, 1, 3] if line else list(reversed(far_first(L)))

    def share(j):
        return rows(j * (T // L), T // L, 16)

    def gather_start(ref, sems):
        out = {}
        for d in [2, 1, 3] if line else far_first(L):
            mine = ref.at[share(me_l)]
            copy = pltpu.make_async_remote_copy(
                src_ref=mine,
                dst_ref=mine,
                send_sem=sems.at[0, d - 1],
                recv_sem=sems.at[1, d - 1],
                device_id={"lab": lab_peers[d - 1]},
                device_id_type=MESH,
            )
            if line and d != 2:
                near = me_l != (3 if d == 1 else 0)
                pl.when(near)(copy.start)
                sent_if.append((near, copy))
            else:
                copy.start()
                sent.append(copy)
            out[d] = copy
        return out

    def relay(ref, sems):
        if not line:
            return
        inner = jnp.logical_or(me_l == 1, me_l == 2)
        block = ref.at[share(lax.rem(me_l + 2, L))]
        end = lax.rem(3 * (me_l + 3), 4)
        copy = pltpu.make_async_remote_copy(
            src_ref=block,
            dst_ref=block,
            send_sem=sems.at[0, L - 1],
            recv_sem=sems.at[1, end * 2 // 3],
            device_id={"lab": end},
            device_id_type=MESH,
        )
        pl.when(inner)(copy.start)
        sent_if.append((inner, copy))

    barrier = pltpu.get_barrier_semaphore()
    for peer in lab_peers:
        pl.semaphore_signal(barrier, inc=1, device_id={"lab": peer}, device_id_type=MESH)
    for peer in seq_peers:
        pl.semaphore_signal(barrier, inc=1, device_id={"seq": peer}, device_id_type=MESH)

    loads = [
        pltpu.make_async_copy(src, dst, load_sem.at[k])
        for k, (src, dst) in enumerate(
            [(proj_h, proj), (hidden_h, hidden), (queries_h, queries), (codew_h, codew)]
        )
    ]
    for load in loads:
        load.start()
    cnt[me_s] = counts[...].astype(F32)
    loads[0].wait()
    loads[1].wait()

    def project(j):
        pre_b[share(j), :] = nn(hidden[share(j), :], proj[...]).astype(BF16)

    lab_order = far_first(L)
    copies = {}
    for k, d in enumerate(lab_order):
        p = lab_peers[d - 1]
        project(p)
        if k == 0:
            pl.semaphore_wait(barrier, S + L - 2)
        copies[d] = send(pre_b.at[share(p)], rs1.at[d - 1], rs1_sem, (d - 1,), {"lab": p})
    project(me_l)
    cnt_copies = [
        send(cnt.at[me_s], cnt.at[me_s], cnt_sem, (d,), {"seq": p})
        for d, p in enumerate(seq_peers)
    ]
    total = pre_b[share(me_l), :].astype(F32)
    for d in reversed(lab_order):
        copies[d].wait_recv()
        total = total + rs1[d - 1].astype(F32)
    lat[share(me_l), :] = jnp.tanh(total).astype(BF16)
    copies = gather_start(lat, ag1_sem)
    loads[2].wait()
    loads[3].wait()

    tc = tile_of(C)
    tot[me_s] = jnp.zeros((2, C), F32)

    def attend(j):
        block = lat[share(j), :]

        @pl.loop(0, C // tc)
        def _(i):
            at = rows(i * tc, tc, tc)
            weights = jnp.exp(nt(block, queries[at, :]))
            values = nt(block, codew[at, :])
            w_s[share(j), at] = weights
            v_s[share(j), at] = values
            tot[me_s, 0:1, at] += jnp.sum(weights, 0, keepdims=True)
            tot[me_s, 1:2, at] += jnp.sum(weights * values, 0, keepdims=True)

    attend(me_l)
    for d in gather_order:
        copies[d].wait_recv()
        if d == 2:
            relay(lat, ag1_sem)
        attend(lax.rem(me_l + L - d, L))

    copies = [
        send(tot.at[me_s], tot.at[me_s], tot_sem, (d,), {"seq": p})
        for d, p in enumerate(seq_peers)
    ]
    latT[...] = lat[...].astype(F32).T.astype(BF16)
    for copy in cnt_copies:
        copy.wait_recv()
    occurrences = jnp.ones((1, C), F32)
    for s in range(S):
        occurrences = occurrences + cnt[s]
    class_weight = (1.0 - balance_beta) / -expm1(occurrences * math.log(balance_beta))
    for copy in copies:
        copy.wait_recv()
    losses = []
    bias_grad = jnp.zeros((1, C), F32)
    for n in range(notes):
        both = jnp.zeros((2, C), F32)
        for s in range(S):
            if s * notes // S == n:
                both = both + tot[s]
        inverse = 1.0 / both[0:1, :]
        mean = both[1:2, :] / both[0:1, :]
        logit = mean + bias[...][None, :]
        y = labels[n : n + 1, :].astype(F32)
        t = jnp.exp(-jnp.abs(logit))
        l1p = jnp.log1p(t)
        big = 1.0 / (1.0 + t)
        small = t / (1.0 + t)
        p = jnp.where(logit >= 0, big, small)
        q = jnp.where(logit >= 0, small, big)
        ls_pos = jnp.minimum(logit, 0.0) - l1p
        ls_neg = jnp.minimum(-logit, 0.0) - l1p
        focal = -(y * q * q * ls_pos + (1.0 - y) * p * p * ls_neg)
        slope = -(
            y * q * q * (q - 2.0 * p * ls_pos)
            + (1.0 - y) * p * p * (2.0 * q * ls_neg - p)
        )
        grad = class_weight * slope
        bias_grad = bias_grad + grad
        den_n[n] = inverse
        mean_n[n] = mean
        grad_n[n] = grad
        losses.append(jnp.sum(focal * class_weight, 1, keepdims=True))
    sc[me_l] = jnp.concatenate(
        [
            jnp.broadcast_to(value, (1, 128))
            for value in [jnp.sum(class_weight, 1, keepdims=True)] + losses
        ],
        axis=0,
    )
    sc_copies = [
        send(sc.at[me_l], sc.at[me_l], sc_sem, (d,), {"lab": p})
        for d, p in enumerate(lab_peers)
    ]

    note = me_s * notes // S
    sister = {"seq": x * 2 + (1 - c)}
    slots = list(range(1, X)) + [0]
    xs = [lax.rem(x + d, X) for d in range(X)]

    def chunk(ref, k):
        size = ref.shape[0] // S
        return rows(k * size, size, 16)

    def stage1(a, part, first):
        out = {}
        for d in slots:
            k = xs[d] * 2 + (1 - c)
            out[d] = send(part.at[chunk(part, k)], first.at[d], st1_sem, (a, d), sister)
        return out

    def stage2(a, part, first, mid, second, arrived):
        out = []
        for d in range(1, X):
            arrived[d].wait_recv()
            mine = part[chunk(part, xs[d] * 2 + c), :].astype(F32)
            mid[d - 1] = (mine + first[d].astype(F32)).astype(BF16)
            out.append(
                send(
                    mid.at[d - 1], second.at[d - 1], st2_sem, (a, d - 1),
                    {"seq": xs[d] * 2 + c},
                )
            )
        return out

    def finish(part, first, second, arrived, copies, scale, out):
        arrived[0].wait_recv()
        total = part[chunk(part, me_s), :].astype(F32) + first[0].astype(F32)
        for d, copy in enumerate(copies):
            copy.wait_recv()
            total = total + second[d].astype(F32)
        out[...] = (total * scale).astype(BF16)

    tw = tile_of(C, 256)

    def code_part(grads, part):
        @pl.loop(0, C // tw)
        def _(i):
            at = rows(i * tw, tw, tw)
            part[at, :] = nn(latT[...], grads[:, at]).T.astype(BF16)

    def latent_grad(j):
        acc[...] = jnp.zeros_like(acc)

        @pl.loop(0, C // tc)
        def _(i):
            at = rows(i * tc, tc, tc)
            value_part = w_s[share(j), at] * den_n[note, :, at] * grad_n[note, :, at]
            score_part = value_part * (v_s[share(j), at] - mean_n[note, :, at])
            vg = value_part.astype(BF16)
            sg = score_part.astype(BF16)
            vg_s[share(j), at] = vg
            sg_s[share(j), at] = sg
            acc[...] += nn(sg, queries[at, :]) + nn(vg, codew[at, :])

    rs2_copies = {}
    for d in lab_order:
        p = lab_peers[d - 1]
        latent_grad(p)
        lg_b[share(p), :] = acc[...].astype(BF16)
        rs2_copies[d] = send(lg_b.at[share(p)], rs2.at[d - 1], rs2_sem, (d - 1,), {"lab": p})
    latent_grad(me_l)
    code_part(vg_s, pw)
    w_first = stage1(1, pw, w1)
    code_part(sg_s, pq)
    q_first = stage1(0, pq, q1)
    w_second = stage2(1, pw, w1, ws, w2, w_first)

    for copy in sc_copies:
        copy.wait_recv()
    scalars = sc[0]
    for j in range(1, L):
        scalars = scalars + sc[j]
    factor = all_codes / scalars[0:1, 0:1]
    loss_out[...] = scalars[1 : 1 + notes, :] * factor
    gb_out[...] = bias_grad * factor

    total = acc[...]
    for d in reversed(lab_order):
        rs2_copies[d].wait_recv()
        total = total + rs2[d - 1].astype(F32)
    wide = lat[share(me_l), :].astype(F32)
    pg[share(me_l), :] = (total * factor * (1.0 - wide * wide)).astype(BF16)
    ag2_copies = gather_start(pg, ag2_sem)
    q_second = stage2(0, pq, q1, qs, q2, q_first)
    for d in gather_order:
        ag2_copies[d].wait_recv()
        if d == 2:
            relay(pg, ag2_sem)
    pgT[...] = pg[...].astype(F32).T.astype(BF16)
    td = tile_of(D, 256)

    @pl.loop(0, D // td)
    def _(i):
        at = rows(i * td, td, td)
        pp[at, :] = nn(pgT[...], hidden[:, at]).T.astype(BF16)

    p_first = stage1(2, pp, p1)

    pg_out[...] = pg[...]
    p_second = stage2(2, pp, p1, ps, p2, p_first)
    finish(pw, w1, w2, w_first, w_second, factor, gw_out)
    finish(pq, q1, q2, q_first, q_second, factor, gq_out)
    finish(pp, p1, p2, p_first, p_second, 1.0, gp_out)
    for copy in sent:
        copy.wait_send()
    for started, copy in sent_if:
        pl.when(started)(copy.wait_send)


def finish_kernel(
    loss, pg, gp, gq, gw, gb, proj, loss_out, gh_out, gp_out, gq_out, gw_out, gb_out, gh, sem
):
    copies = []
    for k, (src, dst) in enumerate([(gp, gp_out), (gq, gq_out), (gw, gw_out)]):
        copies.append(pltpu.make_async_copy(src, dst, sem.at[k]))
        copies[-1].start()
    part = gh.shape[0] // 4
    for k in range(4):
        at = pl.ds(k * part, part)
        gh[at, :] = nt(pg[at, :], proj[...]).astype(BF16)
        copies.append(pltpu.make_async_copy(gh.at[at], gh_out.at[at], sem.at[3 + k]))
        copies[-1].start()
    gb_out[...] = gb[0, :]
    for n in range(loss_out.shape[0]):
        loss_out[n] = jnp.max(loss[n : n + 1, :])
    for copy in copies:
        copy.wait()


def per_device(hidden, proj_weight, queries, code_weight, code_bias, labels, code_counts):
    L = lax.axis_size("lab")
    S = lax.axis_size("seq")
    X = S // 2
    T, D = hidden.shape
    C, E = queries.shape
    notes = labels.shape[0]
    sh = T // L
    vmem = pltpu.VMEM
    dma = pltpu.SemaphoreType.DMA
    scratch = [
        vmem((T, D), BF16),
        vmem((D, E), BF16),
        vmem((C, E), BF16),
        vmem((C, E), BF16),
        dma((4,)),
        vmem((T, E), BF16),
        vmem((L - 1, sh, E), BF16),
        vmem((T, E), BF16),
        vmem((E, T), BF16),
        vmem((T, C), F32),
        vmem((T, C), F32),
        vmem((S, 2, C), F32),
        vmem((S, 1, C), F32),
        vmem((L, 1 + notes, 128), F32),
        vmem((notes, 1, C), F32),
        vmem((notes, 1, C), F32),
        vmem((notes, 1, C), F32),
        vmem((T, C), BF16),
        vmem((T, C), BF16),
        vmem((sh, E), F32),
        vmem((T, E), BF16),
        vmem((L - 1, sh, E), BF16),
        vmem((T, E), BF16),
        vmem((E, T), BF16),
        vmem((C, E), BF16),
        vmem((C, E), BF16),
        vmem((D, E), BF16),
        vmem((X, C // S, E), BF16),
        vmem((X, C // S, E), BF16),
        vmem((X, D // S, E), BF16),
        vmem((X - 1, C // S, E), BF16),
        vmem((X - 1, C // S, E), BF16),
        vmem((X - 1, D // S, E), BF16),
        vmem((X - 1, C // S, E), BF16),
        vmem((X - 1, C // S, E), BF16),
        vmem((X - 1, D // S, E), BF16),
        dma((2, S - 1)),
        dma((2, S - 1)),
        dma((2, L - 1)),
        dma((2, L - 1)),
        dma((2, L)),
        dma((2, L - 1)),
        dma((2, L)),
        dma((2, 3, X)),
        dma((2, 3, X - 1)),
    ]
    whole = pl.BlockSpec(memory_space=pltpu.VMEM)
    anywhere = pl.BlockSpec(memory_space=pl.ANY)
    shapes = dict(
        gp=jax.ShapeDtypeStruct((D // S, E), BF16),
        gq=jax.ShapeDtypeStruct((C // S, E), BF16),
        gw=jax.ShapeDtypeStruct((C // S, E), BF16),
    )
    loss, pg, gp, gq, gw, gb = pl.pallas_call(
        functools.partial(kernel, S, L, float(C * L)),
        out_shape=(
            jax.ShapeDtypeStruct((notes, 128), F32),
            jax.ShapeDtypeStruct((T, E), BF16),
            *shapes.values(),
            jax.ShapeDtypeStruct((1, C), F32),
        ),
        in_specs=[anywhere] * 4 + [whole] * 3,
        out_specs=(whole,) * 6,
        scratch_shapes=scratch,
        compiler_params=pltpu.CompilerParams(
            collective_id=0, has_side_effects=True, vmem_limit_bytes=56 * 1024 * 1024
        ),
    )(hidden, proj_weight, queries, code_weight, code_bias, labels, code_counts)
    return pl.pallas_call(
        finish_kernel,
        out_shape=(
            jax.ShapeDtypeStruct((notes,), F32),
            jax.ShapeDtypeStruct((T, D), BF16),
            *shapes.values(),
            jax.ShapeDtypeStruct((C,), F32),
        ),
        in_specs=[whole] * 7,
        out_specs=(
            pl.BlockSpec(memory_space=pltpu.SMEM),
            anywhere,
            anywhere,
            anywhere,
            anywhere,
            whole,
        ),
        scratch_shapes=[vmem((T, D), BF16), dma((7,))],
    )(loss, pg, gp, gq, gw, gb, proj_weight)


def solution(mesh):
    placed = (
        P(("grp", "seq"), "lab"),
        P("lab", None),
        P("lab", None),
        P("lab", None),
        P("lab"),
        P("grp", "lab"),
        P(("grp", "seq"), "lab"),
    )
    return jax.shard_map(
        per_device,
        mesh=mesh,
        in_specs=placed,
        out_specs=(
            P("grp"),
            P(("grp", "seq"), "lab"),
            P(("grp", "lab", "seq"), None),
            P(("grp", "lab", "seq"), None),
            P(("grp", "lab", "seq"), None),
            P(("grp", "lab")),
        ),
        check_vma=False,
    )
```

```python
import functools
import math

import jax
import jax.numpy as jnp
from jax import lax
from jax.experimental import pallas as pl
from jax.experimental.pallas import tpu as pltpu
from jax.sharding import PartitionSpec as P

balance_beta = 0.9999
MESH = pl.DeviceIdType.MESH
F32 = jnp.float32
BF16 = jnp.bfloat16


def expm1(x):
    series = jnp.ones_like(x)
    for order in range(10, 1, -1):
        series = 1.0 + x * series * (1.0 / order)
    return jnp.where(jnp.abs(x) < 0.5, x * series, jnp.exp(x) - 1.0)


def nt(a, b):
    return lax.dot_general(a, b, (((1,), (1,)), ((), ())), preferred_element_type=F32)


def nn(a, b):
    return jnp.dot(a, b, preferred_element_type=F32)


def rows(start, size, multiple):
    return pl.ds(pl.multiple_of(start, multiple), size)


def tile_of(size, most=768):
    for tile in (768, 512, 256):
        if tile <= most and size % tile == 0:
            return tile
    return size


def far_first(count):
    return sorted(range(1, count), key=lambda d: -min(d, count - d))


def kernel(
    S, L, all_codes,
    hidden_h, proj_h, queries_h, codew_h, bias, labels, counts,
    loss_out, pg_out, gp_out, gq_out, gw_out, gb_out,
    hidden, proj, queries, codew, load_sem, pre_b, rs1, lat, latT, w_s, v_s, tot, cnt, sc, den_n, mean_n, grad_n,
    sg_s, vg_s, acc, lg_b, rs2, pg, pgT,
    pq, pw, pp, q1, w1, p1, qs, ws, ps, q2, w2, p2,
    cnt_sem, tot_sem, sc_sem, rs1_sem, ag1_sem, rs2_sem, ag2_sem, st1_sem, st2_sem,
):
    T, D = hidden.shape
    C, E = queries.shape
    notes = labels.shape[0]
    X = S // 2
    sh = T // L
    me_s = lax.axis_index("seq")
    me_l = lax.axis_index("lab")
    x = me_s // 2
    c = lax.rem(me_s, 2)
    lab_peers = [lax.rem(me_l + d, L) for d in range(1, L)]
    seq_peers = [lax.rem(me_s + d, S) for d in range(1, S)]
    sent = []
    sent_if = []

    def send(src, dst, sems, index, device):
        copy = pltpu.make_async_remote_copy(
            src_ref=src,
            dst_ref=dst,
            send_sem=sems.at[(0,) + index],
            recv_sem=sems.at[(1,) + index],
            device_id=device,
            device_id_type=MESH,
        )
        copy.start()
        sent.append(copy)
        return copy

    line = L == 4
    gather_order = [2, 1, 3] if line else list(reversed(far_first(L)))

    def share(j):
        return rows(j * (T // L), T // L, 16)

    def gather_start(ref, sems):
        out = {}
        for d in [2, 1, 3] if line else far_first(L):
            mine = ref.at[share(me_l)]
            copy = pltpu.make_async_remote_copy(
                src_ref=mine,
                dst_ref=mine,
                send_sem=sems.at[0, d - 1],
                recv_sem=sems.at[1, d - 1],
                device_id={"lab": lab_peers[d - 1]},
                device_id_type=MESH,
            )
            if line and d != 2:
                near = me_l != (3 if d == 1 else 0)
                pl.when(near)(copy.start)
                sent_if.append((near, copy))
            else:
                copy.start()
                sent.append(copy)
            out[d] = copy
        return out

    def relay(ref, sems):
        if not line:
            return
        block = ref.at[share(lax.rem(me_l + 2, L))]
        end = lax.rem(3 * (me_l + 3), 4)
        copy = pltpu.make_async_remote_copy(
            src_ref=block,
            dst_ref=block,
            send_sem=sems.at[0, L - 1],
            recv_sem=sems.at[1, end * 2 // 3],
            device_id={"lab": end},
            device_id_type=MESH,
        )
        pl.when(inner)(copy.start)
        sent_if.append((inner, copy))

    reduce_order = [3, 1, 2] if line else far_first(L)
    inner = jnp.logical_or(me_l == 1, me_l == 2)
    outer = jnp.logical_or(me_l == 0, me_l == L - 1)

    def arrive(slots, sems, k):
        pltpu.make_async_remote_copy(
            src_ref=slots.at[k],
            dst_ref=slots.at[k],
            send_sem=sems.at[0, k],
            recv_sem=sems.at[1, k],
            device_id={"lab": lab_peers[0]},
            device_id_type=MESH,
        ).wait_recv()

    def term_copy(ref, slots, sems, d):
        device, slot = lab_peers[d - 1], d - 1
        if line and d != 2:
            far = me_l // 3 if d == 1 else (3 - me_l) // 3
            device = device * (1 - far) + (2 if d == 1 else 1) * far
            slot = 3 * far if d == 1 else 2 + far
        return pltpu.make_async_remote_copy(
            src_ref=ref.at[share(lab_peers[d - 1])],
            dst_ref=slots.at[slot],
            send_sem=sems.at[0, d - 1],
            recv_sem=sems.at[1, slot],
            device_id={"lab": device},
            device_id_type=MESH,
        )

    def term_send(ref, slots, sems, d):
        copy = term_copy(ref, slots, sems, d)
        if line and d == 2:
            pl.when(outer)(copy.start)
        else:
            copy.start()
        sent.append(copy)

    def term_join(ref, slots, sems):
        if not line:
            return

        @pl.when(inner)
        def _():
            arrive(slots, sems, 3)
            at = share(lab_peers[1])
            ref[at, :] = (ref[at, :].astype(F32) + slots[3].astype(F32)).astype(BF16)
            term_copy(ref, slots, sems, 2).start()

    def term_sum(total, slots, sems):
        for d in [1, 3, 2] if line else reversed(reduce_order):
            if line and d != 2:
                absent = me_l == (0 if d == 1 else 3)

                @pl.when(absent)
                def _():
                    slots[d - 1] = jnp.zeros_like(slots[d - 1])

                @pl.when(jnp.logical_not(absent))
                def _():
                    arrive(slots, sems, d - 1)
            else:
                arrive(slots, sems, d - 1)
            total = total + slots[d - 1].astype(F32)
        return total

    barrier = pltpu.get_barrier_semaphore()
    for peer in lab_peers:
        pl.semaphore_signal(barrier, inc=1, device_id={"lab": peer}, device_id_type=MESH)
    for peer in seq_peers:
        pl.semaphore_signal(barrier, inc=1, device_id={"seq": peer}, device_id_type=MESH)

    loads = [
        pltpu.make_async_copy(src, dst, load_sem.at[k])
        for k, (src, dst) in enumerate(
            [(proj_h, proj), (hidden_h, hidden), (queries_h, queries), (codew_h, codew)]
        )
    ]
    for load in loads:
        load.start()
    cnt[me_s] = counts[...].astype(F32)
    loads[0].wait()
    loads[1].wait()

    def project(j):
        pre_b[share(j), :] = nn(hidden[share(j), :], proj[...]).astype(BF16)

    for k, d in enumerate(reduce_order):
        p = lab_peers[d - 1]
        project(p)
        if k == 0:
            pl.semaphore_wait(barrier, S + L - 2)
        term_send(pre_b, rs1, rs1_sem, d)
    project(me_l)
    term_join(pre_b, rs1, rs1_sem)
    cnt_copies = [
        send(cnt.at[me_s], cnt.at[me_s], cnt_sem, (d,), {"seq": p})
        for d, p in enumerate(seq_peers)
    ]
    total = term_sum(pre_b[share(me_l), :].astype(F32), rs1, rs1_sem)
    lat[share(me_l), :] = jnp.tanh(total).astype(BF16)
    copies = gather_start(lat, ag1_sem)
    loads[2].wait()
    loads[3].wait()

    tc = tile_of(C)
    tot[me_s] = jnp.zeros((2, C), F32)

    def attend(j):
        block = lat[share(j), :]

        @pl.loop(0, C // tc)
        def _(i):
            at = rows(i * tc, tc, tc)
            weights = jnp.exp(nt(block, queries[at, :]))
            values = nt(block, codew[at, :])
            w_s[share(j), at] = weights
            v_s[share(j), at] = values
            tot[me_s, 0:1, at] += jnp.sum(weights, 0, keepdims=True)
            tot[me_s, 1:2, at] += jnp.sum(weights * values, 0, keepdims=True)

    attend(me_l)
    for d in gather_order:
        copies[d].wait_recv()
        if d == 2:
            relay(lat, ag1_sem)
        attend(lax.rem(me_l + L - d, L))

    copies = [
        send(tot.at[me_s], tot.at[me_s], tot_sem, (d,), {"seq": p})
        for d, p in enumerate(seq_peers)
    ]
    latT[...] = lat[...].astype(F32).T.astype(BF16)
    for copy in cnt_copies:
        copy.wait_recv()
    occurrences = jnp.ones((1, C), F32)
    for s in range(S):
        occurrences = occurrences + cnt[s]
    class_weight = (1.0 - balance_beta) / -expm1(occurrences * math.log(balance_beta))
    for copy in copies:
        copy.wait_recv()
    losses = []
    bias_grad = jnp.zeros((1, C), F32)
    for n in range(notes):
        both = jnp.zeros((2, C), F32)
        for s in range(S):
            if s * notes // S == n:
                both = both + tot[s]
        inverse = 1.0 / both[0:1, :]
        mean = both[1:2, :] / both[0:1, :]
        logit = mean + bias[...][None, :]
        y = labels[n : n + 1, :].astype(F32)
        t = jnp.exp(-jnp.abs(logit))
        l1p = jnp.log1p(t)
        big = 1.0 / (1.0 + t)
        small = t / (1.0 + t)
        p = jnp.where(logit >= 0, big, small)
        q = jnp.where(logit >= 0, small, big)
        ls_pos = jnp.minimum(logit, 0.0) - l1p
        ls_neg = jnp.minimum(-logit, 0.0) - l1p
        focal = -(y * q * q * ls_pos + (1.0 - y) * p * p * ls_neg)
        slope = -(
            y * q * q * (q - 2.0 * p * ls_pos)
            + (1.0 - y) * p * p * (2.0 * q * ls_neg - p)
        )
        grad = class_weight * slope
        bias_grad = bias_grad + grad
        den_n[n] = inverse
        mean_n[n] = mean
        grad_n[n] = grad
        losses.append(jnp.sum(focal * class_weight, 1, keepdims=True))
    sc[me_l] = jnp.concatenate(
        [
            jnp.broadcast_to(value, (1, 128))
            for value in [jnp.sum(class_weight, 1, keepdims=True)] + losses
        ],
        axis=0,
    )
    sc_copies = [
        send(sc.at[me_l], sc.at[me_l], sc_sem, (d,), {"lab": p})
        for d, p in enumerate(lab_peers)
    ]

    note = me_s * notes // S
    sister = {"seq": x * 2 + (1 - c)}
    slots = list(range(1, X)) + [0]
    xs = [lax.rem(x + d, X) for d in range(X)]

    def chunk(ref, k):
        size = ref.shape[0] // S
        return rows(k * size, size, 16)

    def stage1(a, part, first):
        out = {}
        for d in slots:
            k = xs[d] * 2 + (1 - c)
            out[d] = send(part.at[chunk(part, k)], first.at[d], st1_sem, (a, d), sister)
        return out

    def stage2(a, part, first, mid, second, arrived):
        out = []
        for d in range(1, X):
            arrived[d].wait_recv()
            mine = part[chunk(part, xs[d] * 2 + c), :].astype(F32)
            mid[d - 1] = (mine + first[d].astype(F32)).astype(BF16)
            out.append(
                send(
                    mid.at[d - 1], second.at[d - 1], st2_sem, (a, d - 1),
                    {"seq": xs[d] * 2 + c},
                )
            )
        return out

    def finish(part, first, second, arrived, copies, scale, out):
        arrived[0].wait_recv()
        total = part[chunk(part, me_s), :].astype(F32) + first[0].astype(F32)
        for d, copy in enumerate(copies):
            copy.wait_recv()
            total = total + second[d].astype(F32)
        out[...] = (total * scale).astype(BF16)

    tw = tile_of(C, 256)

    def code_part(grads, part):
        @pl.loop(0, C // tw)
        def _(i):
            at = rows(i * tw, tw, tw)
            part[at, :] = nn(latT[...], grads[:, at]).T.astype(BF16)

    def latent_grad(j):
        acc[...] = jnp.zeros_like(acc)

        @pl.loop(0, C // tc)
        def _(i):
            at = rows(i * tc, tc, tc)
            value_part = w_s[share(j), at] * den_n[note, :, at] * grad_n[note, :, at]
            score_part = value_part * (v_s[share(j), at] - mean_n[note, :, at])
            vg = value_part.astype(BF16)
            sg = score_part.astype(BF16)
            vg_s[share(j), at] = vg
            sg_s[share(j), at] = sg
            acc[...] += nn(sg, queries[at, :]) + nn(vg, codew[at, :])

    for d in reduce_order:
        p = lab_peers[d - 1]
        latent_grad(p)
        lg_b[share(p), :] = acc[...].astype(BF16)
        term_send(lg_b, rs2, rs2_sem, d)
    latent_grad(me_l)
    term_join(lg_b, rs2, rs2_sem)
    code_part(vg_s, pw)
    w_first = stage1(1, pw, w1)
    code_part(sg_s, pq)
    q_first = stage1(0, pq, q1)
    w_second = stage2(1, pw, w1, ws, w2, w_first)

    for copy in sc_copies:
        copy.wait_recv()
    scalars = sc[0]
    for j in range(1, L):
        scalars = scalars + sc[j]
    factor = all_codes / scalars[0:1, 0:1]
    loss_out[...] = scalars[1 : 1 + notes, :] * factor
    gb_out[...] = bias_grad * factor

    total = term_sum(acc[...], rs2, rs2_sem)
    wide = lat[share(me_l), :].astype(F32)
    pg[share(me_l), :] = (total * factor * (1.0 - wide * wide)).astype(BF16)
    ag2_copies = gather_start(pg, ag2_sem)
    q_second = stage2(0, pq, q1, qs, q2, q_first)
    for d in gather_order:
        ag2_copies[d].wait_recv()
        if d == 2:
            relay(pg, ag2_sem)
    pgT[...] = pg[...].astype(F32).T.astype(BF16)
    td = tile_of(D, 256)

    @pl.loop(0, D // td)
    def _(i):
        at = rows(i * td, td, td)
        pp[at, :] = nn(pgT[...], hidden[:, at]).T.astype(BF16)

    p_first = stage1(2, pp, p1)

    pg_out[...] = pg[...]
    p_second = stage2(2, pp, p1, ps, p2, p_first)
    finish(pw, w1, w2, w_first, w_second, factor, gw_out)
    finish(pq, q1, q2, q_first, q_second, factor, gq_out)
    finish(pp, p1, p2, p_first, p_second, 1.0, gp_out)
    for copy in sent:
        copy.wait_send()
    for started, copy in sent_if:
        pl.when(started)(copy.wait_send)


def finish_kernel(
    loss, pg, gp, gq, gw, gb, proj, loss_out, gh_out, gp_out, gq_out, gw_out, gb_out, gh, sem
):
    copies = []
    for k, (src, dst) in enumerate([(gp, gp_out), (gq, gq_out), (gw, gw_out)]):
        copies.append(pltpu.make_async_copy(src, dst, sem.at[k]))
        copies[-1].start()
    part = gh.shape[0] // 4
    for k in range(4):
        at = pl.ds(k * part, part)
        gh[at, :] = nt(pg[at, :], proj[...]).astype(BF16)
        copies.append(pltpu.make_async_copy(gh.at[at], gh_out.at[at], sem.at[3 + k]))
        copies[-1].start()
    gb_out[...] = gb[0, :]
    for n in range(loss_out.shape[0]):
        loss_out[n] = jnp.max(loss[n : n + 1, :])
    for copy in copies:
        copy.wait()


def per_device(hidden, proj_weight, queries, code_weight, code_bias, labels, code_counts):
    L = lax.axis_size("lab")
    S = lax.axis_size("seq")
    X = S // 2
    T, D = hidden.shape
    C, E = queries.shape
    notes = labels.shape[0]
    sh = T // L
    vmem = pltpu.VMEM
    dma = pltpu.SemaphoreType.DMA
    scratch = [
        vmem((T, D), BF16),
        vmem((D, E), BF16),
        vmem((C, E), BF16),
        vmem((C, E), BF16),
        dma((4,)),
        vmem((T, E), BF16),
        vmem((L, sh, E), BF16),
        vmem((T, E), BF16),
        vmem((E, T), BF16),
        vmem((T, C), F32),
        vmem((T, C), F32),
        vmem((S, 2, C), F32),
        vmem((S, 1, C), F32),
        vmem((L, 1 + notes, 128), F32),
        vmem((notes, 1, C), F32),
        vmem((notes, 1, C), F32),
        vmem((notes, 1, C), F32),
        vmem((T, C), BF16),
        vmem((T, C), BF16),
        vmem((sh, E), F32),
        vmem((T, E), BF16),
        vmem((L, sh, E), BF16),
        vmem((T, E), BF16),
        vmem((E, T), BF16),
        vmem((C, E), BF16),
        vmem((C, E), BF16),
        vmem((D, E), BF16),
        vmem((X, C // S, E), BF16),
        vmem((X, C // S, E), BF16),
        vmem((X, D // S, E), BF16),
        vmem((X - 1, C // S, E), BF16),
        vmem((X - 1, C // S, E), BF16),
        vmem((X - 1, D // S, E), BF16),
        vmem((X - 1, C // S, E), BF16),
        vmem((X - 1, C // S, E), BF16),
        vmem((X - 1, D // S, E), BF16),
        dma((2, S - 1)),
        dma((2, S - 1)),
        dma((2, L - 1)),
        dma((2, L)),
        dma((2, L)),
        dma((2, L)),
        dma((2, L)),
        dma((2, 3, X)),
        dma((2, 3, X - 1)),
    ]
    whole = pl.BlockSpec(memory_space=pltpu.VMEM)
    anywhere = pl.BlockSpec(memory_space=pl.ANY)
    shapes = dict(
        gp=jax.ShapeDtypeStruct((D // S, E), BF16),
        gq=jax.ShapeDtypeStruct((C // S, E), BF16),
        gw=jax.ShapeDtypeStruct((C // S, E), BF16),
    )
    loss, pg, gp, gq, gw, gb = pl.pallas_call(
        functools.partial(kernel, S, L, float(C * L)),
        out_shape=(
            jax.ShapeDtypeStruct((notes, 128), F32),
            jax.ShapeDtypeStruct((T, E), BF16),
            *shapes.values(),
            jax.ShapeDtypeStruct((1, C), F32),
        ),
        in_specs=[anywhere] * 4 + [whole] * 3,
        out_specs=(whole,) * 6,
        scratch_shapes=scratch,
        compiler_params=pltpu.CompilerParams(
            collective_id=0, has_side_effects=True, vmem_limit_bytes=56 * 1024 * 1024
        ),
    )(hidden, proj_weight, queries, code_weight, code_bias, labels, code_counts)
    return pl.pallas_call(
        finish_kernel,
        out_shape=(
            jax.ShapeDtypeStruct((notes,), F32),
            jax.ShapeDtypeStruct((T, D), BF16),
            *shapes.values(),
            jax.ShapeDtypeStruct((C,), F32),
        ),
        in_specs=[whole] * 7,
        out_specs=(
            pl.BlockSpec(memory_space=pltpu.SMEM),
            anywhere,
            anywhere,
            anywhere,
            anywhere,
            whole,
        ),
        scratch_shapes=[vmem((T, D), BF16), dma((7,))],
    )(loss, pg, gp, gq, gw, gb, proj_weight)


def solution(mesh):
    placed = (
        P(("grp", "seq"), "lab"),
        P("lab", None),
        P("lab", None),
        P("lab", None),
        P("lab"),
        P("grp", "lab"),
        P(("grp", "seq"), "lab"),
    )
    return jax.shard_map(
        per_device,
        mesh=mesh,
        in_specs=placed,
        out_specs=(
            P("grp"),
            P(("grp", "seq"), "lab"),
            P(("grp", "lab", "seq"), None),
            P(("grp", "lab", "seq"), None),
            P(("grp", "lab", "seq"), None),
            P(("grp", "lab")),
        ),
        check_vma=False,
    )
```

```python
import functools
import math

import jax
import jax.numpy as jnp
from jax import lax
from jax.experimental import pallas as pl
from jax.experimental.pallas import tpu as pltpu
from jax.sharding import PartitionSpec as P

balance_beta = 0.9999
MESH = pl.DeviceIdType.MESH
F32 = jnp.float32
BF16 = jnp.bfloat16


def expm1(x):
    series = jnp.ones_like(x)
    for order in range(10, 1, -1):
        series = 1.0 + x * series * (1.0 / order)
    return jnp.where(jnp.abs(x) < 0.5, x * series, jnp.exp(x) - 1.0)


def nt(a, b):
    return lax.dot_general(a, b, (((1,), (1,)), ((), ())), preferred_element_type=F32)


def nn(a, b):
    return jnp.dot(a, b, preferred_element_type=F32)


def rows(start, size, multiple):
    return pl.ds(pl.multiple_of(start, multiple), size)


def tile_of(size, most=768):
    for tile in (768, 512, 256):
        if tile <= most and size % tile == 0:
            return tile
    return size


def far_first(count):
    return sorted(range(1, count), key=lambda d: -min(d, count - d))


def kernel(
    S, L, all_codes,
    hidden_h, proj_h, queries_h, codew_h, bias, labels, counts,
    loss_out, pg_out, gp_out, gq_out, gw_out, gb_out,
    hidden, proj, queries, codew, load_sem, pre_b, rs1, lat, latT, w_s, v_s, tot, cnt, sc, den_n, mean_n, grad_n,
    sg_s, vg_s, acc, lg_b, rs2, pg, pgT,
    pq, pw, pp, q1, w1, p1, qs, ws, ps, q2, w2, p2,
    cnt_sem, tot_sem, sc_sem, rs1_sem, ag1_sem, rs2_sem, ag2_sem, st1_sem, st2_sem,
):
    T, D = hidden.shape
    C, E = queries.shape
    notes = labels.shape[0]
    X = S // 2
    sh = T // L
    me_s = lax.axis_index("seq")
    me_l = lax.axis_index("lab")
    x = me_s // 2
    c = lax.rem(me_s, 2)
    lab_peers = [lax.rem(me_l + d, L) for d in range(1, L)]
    seq_peers = [lax.rem(me_s + d, S) for d in range(1, S)]
    sent = []
    sent_if = []

    def send(src, dst, sems, index, device):
        copy = pltpu.make_async_remote_copy(
            src_ref=src,
            dst_ref=dst,
            send_sem=sems.at[(0,) + index],
            recv_sem=sems.at[(1,) + index],
            device_id=device,
            device_id_type=MESH,
        )
        copy.start()
        sent.append(copy)
        return copy

    line = L == 4
    gather_order = [2, 1, 3] if line else list(reversed(far_first(L)))

    def share(j):
        return rows(j * (T // L), T // L, 16)

    def gather_start(ref, sems):
        out = {}
        for d in [2, 1, 3] if line else far_first(L):
            mine = ref.at[share(me_l)]
            copy = pltpu.make_async_remote_copy(
                src_ref=mine,
                dst_ref=mine,
                send_sem=sems.at[0, d - 1],
                recv_sem=sems.at[1, d - 1],
                device_id={"lab": lab_peers[d - 1]},
                device_id_type=MESH,
            )
            if line and d != 2:
                near = me_l != (3 if d == 1 else 0)
                pl.when(near)(copy.start)
                sent_if.append((near, copy))
            else:
                copy.start()
                sent.append(copy)
            out[d] = copy
        return out

    def relay(ref, sems):
        if not line:
            return
        inner = jnp.logical_or(me_l == 1, me_l == 2)
        block = ref.at[share(lax.rem(me_l + 2, L))]
        end = lax.rem(3 * (me_l + 3), 4)
        copy = pltpu.make_async_remote_copy(
            src_ref=block,
            dst_ref=block,
            send_sem=sems.at[0, L - 1],
            recv_sem=sems.at[1, end * 2 // 3],
            device_id={"lab": end},
            device_id_type=MESH,
        )
        pl.when(inner)(copy.start)
        sent_if.append((inner, copy))

    barrier = pltpu.get_barrier_semaphore()
    for peer in lab_peers:
        pl.semaphore_signal(barrier, inc=1, device_id={"lab": peer}, device_id_type=MESH)
    for peer in seq_peers:
        pl.semaphore_signal(barrier, inc=1, device_id={"seq": peer}, device_id_type=MESH)

    loads = [
        pltpu.make_async_copy(src, dst, load_sem.at[k])
        for k, (src, dst) in enumerate(
            [(proj_h, proj), (hidden_h, hidden), (queries_h, queries), (codew_h, codew)]
        )
    ]
    for load in loads:
        load.start()
    cnt[me_s] = counts[...].astype(F32)
    loads[0].wait()
    loads[1].wait()

    def project(j):
        pre_b[share(j), :] = nn(hidden[share(j), :], proj[...]).astype(BF16)

    lab_order = far_first(L)
    copies = {}
    for k, d in enumerate(lab_order):
        p = lab_peers[d - 1]
        project(p)
        if k == 0:
            pl.semaphore_wait(barrier, S + L - 2)
        copies[d] = send(pre_b.at[share(p)], rs1.at[d - 1], rs1_sem, (d - 1,), {"lab": p})
    project(me_l)
    cnt_copies = [
        send(cnt.at[me_s], cnt.at[me_s], cnt_sem, (d,), {"seq": p})
        for d, p in enumerate(seq_peers)
    ]
    total = pre_b[share(me_l), :].astype(F32)
    for d in reversed(lab_order):
        copies[d].wait_recv()
        total = total + rs1[d - 1].astype(F32)
    lat[share(me_l), :] = jnp.tanh(total).astype(BF16)
    copies = gather_start(lat, ag1_sem)
    loads[2].wait()
    loads[3].wait()

    tc = tile_of(C)
    tot[me_s] = jnp.zeros((2, C), F32)

    def attend(j):
        block = lat[share(j), :]

        @pl.loop(0, C // tc)
        def _(i):
            at = rows(i * tc, tc, tc)
            weights = jnp.exp(nt(block, queries[at, :]))
            values = nt(block, codew[at, :])
            w_s[share(j), at] = weights
            v_s[share(j), at] = values
            tot[me_s, 0:1, at] += jnp.sum(weights, 0, keepdims=True)
            tot[me_s, 1:2, at] += jnp.sum(weights * values, 0, keepdims=True)

    attend(me_l)
    for d in gather_order:
        copies[d].wait_recv()
        if d == 2:
            relay(lat, ag1_sem)
        attend(lax.rem(me_l + L - d, L))

    copies = [
        send(tot.at[me_s], tot.at[me_s], tot_sem, (d,), {"seq": p})
        for d, p in enumerate(seq_peers)
    ]
    latT[...] = lat[...].astype(F32).T.astype(BF16)
    for copy in cnt_copies:
        copy.wait_recv()
    occurrences = jnp.ones((1, C), F32)
    for s in range(S):
        occurrences = occurrences + cnt[s]
    class_weight = (1.0 - balance_beta) / -expm1(occurrences * math.log(balance_beta))
    for copy in copies:
        copy.wait_recv()
    losses = []
    bias_grad = jnp.zeros((1, C), F32)
    for n in range(notes):
        both = jnp.zeros((2, C), F32)
        for s in range(S):
            if s * notes // S == n:
                both = both + tot[s]
        inverse = 1.0 / both[0:1, :]
        mean = both[1:2, :] / both[0:1, :]
        logit = mean + bias[...][None, :]
        y = labels[n : n + 1, :].astype(F32)
        t = jnp.exp(-jnp.abs(logit))
        l1p = jnp.log1p(t)
        big = 1.0 / (1.0 + t)
        small = t / (1.0 + t)
        p = jnp.where(logit >= 0, big, small)
        q = jnp.where(logit >= 0, small, big)
        ls_pos = jnp.minimum(logit, 0.0) - l1p
        ls_neg = jnp.minimum(-logit, 0.0) - l1p
        focal = -(y * q * q * ls_pos + (1.0 - y) * p * p * ls_neg)
        slope = -(
            y * q * q * (q - 2.0 * p * ls_pos)
            + (1.0 - y) * p * p * (2.0 * q * ls_neg - p)
        )
        grad = class_weight * slope
        bias_grad = bias_grad + grad
        den_n[n] = inverse
        mean_n[n] = mean
        grad_n[n] = grad
        losses.append(jnp.sum(focal * class_weight, 1, keepdims=True))
    sc[me_l] = jnp.concatenate(
        [
            jnp.broadcast_to(value, (1, 128))
            for value in [jnp.sum(class_weight, 1, keepdims=True)] + losses
        ],
        axis=0,
    )
    sc_copies = [
        send(sc.at[me_l], sc.at[me_l], sc_sem, (d,), {"lab": p})
        for d, p in enumerate(lab_peers)
    ]

    note = me_s * notes // S
    sister = {"seq": x * 2 + (1 - c)}
    slots = list(range(1, X)) + [0]
    xs = [lax.rem(x + d, X) for d in range(X)]

    def chunk(ref, k):
        size = ref.shape[0] // S
        return rows(k * size, size, 16)

    def stage1(a, part, first):
        out = {}
        for d in slots:
            k = xs[d] * 2 + (1 - c)
            out[d] = send(part.at[chunk(part, k)], first.at[d], st1_sem, (a, d), sister)
        return out

    def stage2(a, part, first, mid, second, arrived):
        out = []
        for d in range(1, X):
            arrived[d].wait_recv()
            mine = part[chunk(part, xs[d] * 2 + c), :].astype(F32)
            mid[d - 1] = (mine + first[d].astype(F32)).astype(BF16)
            out.append(
                send(
                    mid.at[d - 1], second.at[d - 1], st2_sem, (a, d - 1),
                    {"seq": xs[d] * 2 + c},
                )
            )
        return out

    def finish(part, first, second, arrived, copies, scale, out):
        arrived[0].wait_recv()
        total = part[chunk(part, me_s), :].astype(F32) + first[0].astype(F32)
        for d, copy in enumerate(copies):
            copy.wait_recv()
            total = total + second[d].astype(F32)
        out[...] = (total * scale).astype(BF16)

    tw = tile_of(C, 256)

    def code_part(grads, part):
        @pl.loop(0, C // tw)
        def _(i):
            at = rows(i * tw, tw, tw)
            part[at, :] = nn(latT[...], grads[:, at]).T.astype(BF16)

    def latent_grad(j):
        acc[...] = jnp.zeros_like(acc)

        @pl.loop(0, C // tc)
        def _(i):
            at = rows(i * tc, tc, tc)
            value_part = w_s[share(j), at] * den_n[note, :, at] * grad_n[note, :, at]
            score_part = value_part * (v_s[share(j), at] - mean_n[note, :, at])
            vg = value_part.astype(BF16)
            sg = score_part.astype(BF16)
            vg_s[share(j), at] = vg
            sg_s[share(j), at] = sg
            acc[...] += nn(sg, queries[at, :]) + nn(vg, codew[at, :])

    rs2_copies = {}
    for d in lab_order:
        p = lab_peers[d - 1]
        latent_grad(p)
        lg_b[share(p), :] = acc[...].astype(BF16)
        rs2_copies[d] = send(lg_b.at[share(p)], rs2.at[d - 1], rs2_sem, (d - 1,), {"lab": p})
    latent_grad(me_l)
    code_part(vg_s, pw)
    w_first = stage1(1, pw, w1)
    code_part(sg_s, pq)
    q_first = stage1(0, pq, q1)
    w_second = stage2(1, pw, w1, ws, w2, w_first)

    for copy in sc_copies:
        copy.wait_recv()
    scalars = sc[0]
    for j in range(1, L):
        scalars = scalars + sc[j]
    factor = all_codes / scalars[0:1, 0:1]
    loss_out[...] = scalars[1 : 1 + notes, :] * factor
    gb_out[...] = bias_grad * factor

    total = acc[...]
    for d in reversed(lab_order):
        rs2_copies[d].wait_recv()
        total = total + rs2[d - 1].astype(F32)
    wide = lat[share(me_l), :].astype(F32)
    pg[share(me_l), :] = (total * factor * (1.0 - wide * wide)).astype(BF16)
    ag2_copies = gather_start(pg, ag2_sem)
    q_second = stage2(0, pq, q1, qs, q2, q_first)
    for d in gather_order:
        ag2_copies[d].wait_recv()
        if d == 2:
            relay(pg, ag2_sem)
    pgT[...] = pg[...].astype(F32).T.astype(BF16)
    td = D // S if (D // S) % 128 == 0 else D

    def proj_part(start):
        at = rows(start, td, td)
        pp[at, :] = nn(pgT[...], hidden[:, at]).T.astype(BF16)

    if td == D:
        proj_part(0)
        p_first = stage1(2, pp, p1)
    else:
        p_first = {}
        for d in slots:
            k = xs[d] * 2 + (1 - c)
            proj_part(k * td)
            p_first[d] = send(pp.at[chunk(pp, k)], p1.at[d], st1_sem, (2, d), sister)
        for d in slots:
            proj_part((xs[d] * 2 + c) * td)
    pg_out[...] = pg[...]
    p_second = stage2(2, pp, p1, ps, p2, p_first)
    finish(pw, w1, w2, w_first, w_second, factor, gw_out)
    finish(pq, q1, q2, q_first, q_second, factor, gq_out)
    finish(pp, p1, p2, p_first, p_second, 1.0, gp_out)
    for copy in sent:
        copy.wait_send()
    for started, copy in sent_if:
        pl.when(started)(copy.wait_send)


def finish_kernel(
    loss, pg, gp, gq, gw, gb, proj, loss_out, gh_out, gp_out, gq_out, gw_out, gb_out, gh, sem
):
    copies = []
    for k, (src, dst) in enumerate([(gp, gp_out), (gq, gq_out), (gw, gw_out)]):
        copies.append(pltpu.make_async_copy(src, dst, sem.at[k]))
        copies[-1].start()
    part = gh.shape[0] // 4
    for k in range(4):
        at = pl.ds(k * part, part)
        gh[at, :] = nt(pg[at, :], proj[...]).astype(BF16)
        copies.append(pltpu.make_async_copy(gh.at[at], gh_out.at[at], sem.at[3 + k]))
        copies[-1].start()
    gb_out[...] = gb[0, :]
    for n in range(loss_out.shape[0]):
        loss_out[n] = jnp.max(loss[n : n + 1, :])
    for copy in copies:
        copy.wait()


def per_device(hidden, proj_weight, queries, code_weight, code_bias, labels, code_counts):
    L = lax.axis_size("lab")
    S = lax.axis_size("seq")
    X = S // 2
    T, D = hidden.shape
    C, E = queries.shape
    notes = labels.shape[0]
    sh = T // L
    vmem = pltpu.VMEM
    dma = pltpu.SemaphoreType.DMA
    scratch = [
        vmem((T, D), BF16),
        vmem((D, E), BF16),
        vmem((C, E), BF16),
        vmem((C, E), BF16),
        dma((4,)),
        vmem((T, E), BF16),
        vmem((L - 1, sh, E), BF16),
        vmem((T, E), BF16),
        vmem((E, T), BF16),
        vmem((T, C), F32),
        vmem((T, C), F32),
        vmem((S, 2, C), F32),
        vmem((S, 1, C), F32),
        vmem((L, 1 + notes, 128), F32),
        vmem((notes, 1, C), F32),
        vmem((notes, 1, C), F32),
        vmem((notes, 1, C), F32),
        vmem((T, C), BF16),
        vmem((T, C), BF16),
        vmem((sh, E), F32),
        vmem((T, E), BF16),
        vmem((L - 1, sh, E), BF16),
        vmem((T, E), BF16),
        vmem((E, T), BF16),
        vmem((C, E), BF16),
        vmem((C, E), BF16),
        vmem((D, E), BF16),
        vmem((X, C // S, E), BF16),
        vmem((X, C // S, E), BF16),
        vmem((X, D // S, E), BF16),
        vmem((X - 1, C // S, E), BF16),
        vmem((X - 1, C // S, E), BF16),
        vmem((X - 1, D // S, E), BF16),
        vmem((X - 1, C // S, E), BF16),
        vmem((X - 1, C // S, E), BF16),
        vmem((X - 1, D // S, E), BF16),
        dma((2, S - 1)),
        dma((2, S - 1)),
        dma((2, L - 1)),
        dma((2, L - 1)),
        dma((2, L)),
        dma((2, L - 1)),
        dma((2, L)),
        dma((2, 3, X)),
        dma((2, 3, X - 1)),
    ]
    whole = pl.BlockSpec(memory_space=pltpu.VMEM)
    anywhere = pl.BlockSpec(memory_space=pl.ANY)
    shapes = dict(
        gp=jax.ShapeDtypeStruct((D // S, E), BF16),
        gq=jax.ShapeDtypeStruct((C // S, E), BF16),
        gw=jax.ShapeDtypeStruct((C // S, E), BF16),
    )
    loss, pg, gp, gq, gw, gb = pl.pallas_call(
        functools.partial(kernel, S, L, float(C * L)),
        out_shape=(
            jax.ShapeDtypeStruct((notes, 128), F32),
            jax.ShapeDtypeStruct((T, E), BF16),
            *shapes.values(),
            jax.ShapeDtypeStruct((1, C), F32),
        ),
        in_specs=[anywhere] * 4 + [whole] * 3,
        out_specs=(whole,) * 6,
        scratch_shapes=scratch,
        compiler_params=pltpu.CompilerParams(
            collective_id=0, has_side_effects=True, vmem_limit_bytes=56 * 1024 * 1024
        ),
    )(hidden, proj_weight, queries, code_weight, code_bias, labels, code_counts)
    return pl.pallas_call(
        finish_kernel,
        out_shape=(
            jax.ShapeDtypeStruct((notes,), F32),
            jax.ShapeDtypeStruct((T, D), BF16),
            *shapes.values(),
            jax.ShapeDtypeStruct((C,), F32),
        ),
        in_specs=[whole] * 7,
        out_specs=(
            pl.BlockSpec(memory_space=pltpu.SMEM),
            anywhere,
            anywhere,
            anywhere,
            anywhere,
            whole,
        ),
        scratch_shapes=[vmem((T, D), BF16), dma((7,))],
    )(loss, pg, gp, gq, gw, gb, proj_weight)


def solution(mesh):
    placed = (
        P(("grp", "seq"), "lab"),
        P("lab", None),
        P("lab", None),
        P("lab", None),
        P("lab"),
        P("grp", "lab"),
        P(("grp", "seq"), "lab"),
    )
    return jax.shard_map(
        per_device,
        mesh=mesh,
        in_specs=placed,
        out_specs=(
            P("grp"),
            P(("grp", "seq"), "lab"),
            P(("grp", "lab", "seq"), None),
            P(("grp", "lab", "seq"), None),
            P(("grp", "lab", "seq"), None),
            P(("grp", "lab")),
        ),
        check_vma=False,
    )
```
